256 devices in a mesh: section: 64 (over x, y, z_hi, core), kv: 4 (over z_lo).
Axes of the slice: x: 4, y: 4, z: 8 (z_hi: 2, z_lo: 4; z = z_hi * 4 + z_lo), core: 2. Of those that a mesh axis runs over, the one named last changes fastest.
Arguments:
- query: bfloat16 [64, 512, 4096], P('section', None, 'kv'), parts along dimension 2, may hold values from -6 to 6
- grad_output: bfloat16 [64, 512, 4096], P('section', None, 'kv'), parts along dimension 2, may hold values from -150 to 150
- log_total: bfloat16 [64, 512, 32], P('section', None, 'kv'), parts along dimension 2, may hold values from -1 to 10, as said below
- offset: bfloat16 [64, 512, 32], P('section', None, 'kv'), parts along dimension 2, may hold values from -600 to 600
- slice_keys: bfloat16 [64, 512, 1024], P('section', None, 'kv'), parts along dimension 2, may hold values from -7 to 7
- pool_keys: bfloat16 [64, 1536, 1024], P('section', None, 'kv'), parts along dimension 2, may hold values from -7 to 7
- block_table: int32 [64, 3], P('section'), may hold values from 0 to 2, each once within a row
Outputs:
- query_grad: bfloat16 [64, 512, 4096], P('section', None, 'kv'), parts along dimension 2
- slice_grad: bfloat16 [64, 512, 1024], P('section', None, 'kv'), parts along dimension 2
- pool_grad: bfloat16 [64, 1536, 1024], P('section', None, 'kv'), parts along dimension 2
The draws below stay inside these ranges and needn't reach their ends.
There are 4 independent parts, one for each index of `kv`. The reference program is written for one: setup_inputs(seed, part) draws one part's arguments, and reference() takes and returns one part's arrays. A program takes and returns all parts, laid end to end along the dimension named above; an argument that names none is the same for every part. Nothing has to cross between parts.
Inputs may be any that keep to these rules, and one draw needn't show every extreme that they name: Each row of block_table names every slot 0 to 2 once. log_total lies near the log of the count of visible keys of the row plus one half.
All inputs are finite; a program needn't handle non-finite values.
Results may differ from the reference program's by a relative error of at most 0.0051.
Values may be sent and summed in bfloat16 or wider, within the bound.
No kernel may reach another device: no remote copies, remote signals or barrier semaphores. Data moves between devices by JAX's collectives and lax.ppermute only.
A program may use at most 128 MiB of HBM per device.

```python
import jax
import jax.numpy as jnp
from jax import lax

HQ = 8
DH = 128
BLK = 512
NSL = 4
POOL = 3
LAYERS = 64


def draw_log_total(key, part):
    second_key = jax.random.fold_in(jax.random.fold_in(key, 17), 1)
    layer_ids = jnp.arange(LAYERS, dtype=jnp.int32)[:, None, None]
    slice_depth = NSL - 1 - layer_ids // (LAYERS // NSL) % (NSL - 1)
    row_ids = jnp.arange(BLK, dtype=jnp.int32)[None, :, None]
    visible = (slice_depth * BLK + row_ids + 1).astype(jnp.float32)
    noise = jax.random.uniform(second_key, (LAYERS, BLK, HQ), jnp.float32, -1.0, 1.0)
    return (jnp.log(visible) + 0.5 + noise).astype(jnp.bfloat16)


def block_scale(key, dims, cuts, low, largest):
    factor_of = 1.0
    for dim, blocks in cuts:
        draws = jax.random.uniform(jax.random.fold_in(jax.random.fold_in(key, 6), dim), (blocks,), jnp.float32, low / len(cuts), largest / len(cuts))
        factor_of = factor_of * jnp.repeat(jnp.exp(draws), dims[dim] // blocks).reshape((-1,) + (1,) * (len(dims) - 1 - dim))
    return factor_of


def centred(key, dims, scale, bound, shards=(), kind=jnp.bfloat16):
    array = scale * jax.random.normal(key, dims, jnp.float32)
    if shards:
        array = array * block_scale(key, dims, shards, -0.22, 0.18)
    return jnp.clip(array, -bound, bound).astype(kind)


def setup_inputs(seed: int = 0, part: int = 0) -> dict:
    streams_of = jax.random.split(jax.random.key(seed), 8)
    own_keys = jax.random.split(jax.random.fold_in(streams_of[7], part), 8)
    return {
        "query": centred(own_keys[0], (LAYERS, BLK, HQ * DH), 1.0, 6.0, ((0, 64),)),
        "grad_output": centred(own_keys[1], (LAYERS, BLK, HQ * DH), 25.0, 150.0, ((0, 64),)),
        "log_total": draw_log_total(jax.random.fold_in(jax.random.fold_in(streams_of[7], part), 71), part),
        "offset": centred(own_keys[3], (LAYERS, BLK, HQ), 100.0, 600.0, ((0, 64),)),
        "slice_keys": centred(own_keys[4], (LAYERS, BLK, 2 * DH), 1.2, 7.0, ((0, 64),)),
        "pool_keys": centred(own_keys[5], (LAYERS, POOL * BLK, 2 * DH), 1.2, 7.0, ((0, 64),)),
        "block_table": jax.vmap(lambda own: jax.random.permutation(own, POOL))(jax.random.split(streams_of[6], LAYERS)).reshape((LAYERS, POOL)).astype(jnp.int32),
    }


def block_terms(queries, out_grads, totals, offsets, key_data, value_data, causal):
    score_scale = DH ** -0.5
    scores = jnp.einsum("rhd,cd->rhc", queries.astype(jnp.float32), key_data.astype(jnp.float32)) * score_scale
    weights = jnp.exp(scores - totals.astype(jnp.float32)[:, :, None])
    if causal:
        row_ids = jnp.arange(queries.shape[0], dtype=jnp.int32)
        visible = row_ids[:, None] >= row_ids[None, :]
        weights = jnp.where(visible[:, None, :], weights, jnp.zeros_like(weights))
    weight_grad = jnp.einsum("rhd,cd->rhc", out_grads.astype(jnp.float32), value_data.astype(jnp.float32))
    score_grad = weights * (weight_grad - offsets.astype(jnp.float32)[:, :, None])
    weights_low, score_low = lax.optimization_barrier((weights.astype(jnp.bfloat16), score_grad.astype(jnp.bfloat16)))
    query_part = jnp.einsum("rhc,cd->rhd", score_low.astype(jnp.float32), key_data.astype(jnp.float32)) * score_scale
    key_part = jnp.einsum("rhc,rhd->cd", score_low.astype(jnp.float32), queries.astype(jnp.float32)) * score_scale
    value_part = jnp.einsum("rhc,rhd->cd", weights_low.astype(jnp.float32), out_grads.astype(jnp.float32))
    return query_part, jnp.concatenate([key_part, value_part], axis=1)


def reference(query, grad_output, log_total, offset, slice_keys, pool_keys, block_table):
    group_size = LAYERS // NSL
    half_layers = LAYERS // 2

    def one_layer(layer_index):
        slice_depth = (NSL - 1) - (layer_index // group_size) % (NSL - 1)
        holder = (layer_index + half_layers) % LAYERS
        queries = query[layer_index].reshape(BLK, HQ, DH)
        out_grads = grad_output[layer_index].reshape(BLK, HQ, DH)
        totals = log_total[layer_index]
        offsets = offset[layer_index]
        own_block = slice_keys[layer_index]
        pool_block = pool_keys[holder]
        own_query, own_grad = block_terms(queries, out_grads, totals, offsets, own_block[:, :DH], own_block[:, DH:], True)
        pool_query = jnp.zeros((BLK, HQ, DH), jnp.float32)
        pool_sum = jnp.zeros((POOL * BLK, 2 * DH), jnp.float32)
        for position in range(POOL):
            pool_slot = block_table[holder, position]
            row_start = (pool_slot * BLK).astype(jnp.int32)
            key_block = lax.dynamic_slice_in_dim(pool_block, row_start, BLK, 0)
            query_part, block_grad = block_terms(queries, out_grads, totals, offsets, key_block[:, :DH], key_block[:, DH:], False)
            in_use = (position < slice_depth).astype(jnp.float32)
            pool_query = pool_query + in_use * query_part
            pool_sum = lax.dynamic_update_slice_in_dim(pool_sum, in_use * block_grad, row_start, 0)
        pool_term = lax.optimization_barrier(pool_query.astype(jnp.bfloat16)).astype(jnp.float32)
        query_sum = own_query + pool_term
        return (query_sum.reshape(BLK, HQ * DH).astype(jnp.bfloat16), own_grad.astype(jnp.bfloat16), pool_sum.astype(jnp.bfloat16))

    layers = jnp.arange(LAYERS, dtype=jnp.int32)
    query_grad, slice_grad, pool_sums = lax.map(one_layer, layers)
    pool_grad = jnp.roll(pool_sums, half_layers, axis=0)
    return query_grad, slice_grad, pool_grad
```

```python
import functools

import jax
import jax.numpy as jnp
from jax import lax
from jax.experimental import pallas as pl
from jax.experimental.pallas import tpu as pltpu
from jax.sharding import PartitionSpec as P


NSL = 4
LOG2E = 1.4426950408889634
F32 = jnp.float32
BF16 = jnp.bfloat16
VMEM = pl.BlockSpec(memory_space=pltpu.VMEM)
SMEM = pl.BlockSpec(memory_space=pltpu.SMEM)
HBM = pl.BlockSpec(memory_space=pltpu.HBM)
PIECES = ((0, 0, 512), (1, 0, 512), (2, 0, 512))


def dot(a, b, ca, cb):
    return lax.dot_general(a, b, (((ca,), (cb,)), ((), ())), preferred_element_type=F32)


def in_hbm(x):
    return pltpu.with_memory_space_constraint(x, pltpu.HBM)


def params(mib):
    return pltpu.CompilerParams(vmem_limit_bytes=mib << 20)


def cost(rows, keys, heads, dh):
    return pl.CostEstimate(
        flops=10 * rows * keys * heads * dh, bytes_accessed=1 << 20, transcendentals=rows * keys * heads
    )


def pick_kernel(rows, table_ref, pool_ref, *refs):
    outs, sem = refs[:-1], refs[-1]
    copies = []
    for i, (block, first, size) in enumerate(PIECES):
        at = pl.multiple_of(table_ref[block] * rows + first, 128)
        copies.append(pltpu.make_async_copy(pool_ref.at[pl.ds(at, size), :], outs[i], sem.at[i]))
    for c in copies:
        c.start()
    for c in copies:
        c.wait()


def pick(table, pool, rows):
    width = pool.shape[1]
    return pl.pallas_call(
        functools.partial(pick_kernel, rows),
        in_specs=[SMEM, HBM],
        out_specs=[VMEM] * len(PIECES),
        out_shape=[jax.ShapeDtypeStruct((size, width), pool.dtype) for _, _, size in PIECES],
        scratch_shapes=[pltpu.SemaphoreType.DMA((len(PIECES),))],
        compiler_params=params(4),
        name="pick",
    )(table, in_hbm(pool))


def own_kernel(heads, dh, scale, q_hbm, do_hbm, l_hbm, o_hbm, kv_hbm, dq_ref, g_ref, lt_ref, ot_ref, q_ref, do_ref, l_ref, o_ref, kv_ref, kt_ref, dk_ref, dv_ref, sem):
    rows, width = q_ref.shape
    half = rows // 2
    wide = width // 2
    small = [
        pltpu.make_async_copy(a, b, sem.at[i]) for i, (a, b) in enumerate(((l_hbm, l_ref), (o_hbm, o_ref), (kv_hbm, kv_ref)))
    ]
    large = [
        [
            pltpu.make_async_copy(a.at[:, pl.ds(i * wide, wide)], b.at[:, pl.ds(i * wide, wide)], sem.at[3 + 2 * i + j])
            for j, (a, b) in enumerate(((q_hbm, q_ref), (do_hbm, do_ref)))
        ]
        for i in range(2)
    ]
    for c in small + large[0] + large[1]:
        c.start()
    dk_ref[...] = jnp.zeros_like(dk_ref)
    dv_ref[...] = jnp.zeros_like(dv_ref)
    for c in small:
        c.wait()
    lt_ref[...] = l_ref[...].astype(F32) * LOG2E
    ot_ref[...] = o_ref[...].astype(F32)
    kt_ref[...] = kv_ref[:, :dh].astype(F32).T.astype(BF16)
    key_ids = lax.broadcasted_iota(jnp.int32, (half, half), 0)
    row_ids = lax.broadcasted_iota(jnp.int32, (half, half), 1)
    visible = key_ids <= row_ids
    for h in range(heads):
        if h % (heads // 2) == 0:
            for c in large[h // (heads // 2)]:
                c.wait()
        hs = slice(h * dh, (h + 1) * dh)
        for t in range(2):
            ks = slice(t * half, (t + 1) * half)
            rs = slice(t * half, rows)
            q, do = q_ref[rs, hs], do_ref[rs, hs]
            k, v = kv_ref[ks, :dh], kv_ref[ks, dh:]
            p = jnp.exp2(dot(k, q, 1, 1) * (scale * LOG2E) - lt_ref[h : h + 1, rs])
            first = jnp.where(visible, p[:, :half], 0.0)
            p = first if t == 1 else jnp.concatenate([first, p[:, half:]], axis=1)
            ds = (p * (dot(v, do, 1, 1) - ot_ref[h : h + 1, rs])).astype(BF16)
            dk_ref[ks, :] += dot(ds, q, 1, 0)
            dv_ref[ks, :] += dot(p.astype(BF16), do, 1, 0)
            part = dot(kt_ref[:, ks], ds, 1, 0)
            if t == 0:
                dq_ref[hs, :] = part
            else:
                dq_ref[hs, rs] += part
    g_ref[:, :dh] = (dk_ref[...] * scale).astype(BF16)
    g_ref[:, dh:] = dv_ref[...].astype(BF16)


def own(q, do, totals, offsets, kv):
    rows, width = q.shape
    heads = totals.shape[0]
    dh = width // heads
    return pl.pallas_call(
        functools.partial(own_kernel, heads, dh, dh**-0.5),
        in_specs=[HBM] * 5,
        out_specs=[VMEM] * 6,
        out_shape=[
            jax.ShapeDtypeStruct((width, rows), F32),
            jax.ShapeDtypeStruct((rows, 2 * dh), BF16),
            jax.ShapeDtypeStruct((heads, rows), F32),
            jax.ShapeDtypeStruct((heads, rows), F32),
            jax.ShapeDtypeStruct((rows, width), BF16),
            jax.ShapeDtypeStruct((rows, width), BF16),
        ],
        scratch_shapes=[
            pltpu.VMEM((heads, rows), BF16),
            pltpu.VMEM((heads, rows), BF16),
            pltpu.VMEM((rows, 2 * dh), BF16),
            pltpu.VMEM((dh, rows), BF16),
            pltpu.VMEM((rows, dh), F32),
            pltpu.VMEM((rows, dh), F32),
            pltpu.SemaphoreType.DMA((7,)),
        ],
        compiler_params=params(20),
        cost_estimate=cost(rows, rows * 3 // 4, heads, dh),
        name="own",
    )(*(in_hbm(x) for x in (q, do, totals, offsets, kv)))


def piece_kernel(heads, dh, scale, block, first, *refs):
    if first:
        depth_ref, q_ref, do_ref, lt_ref, ot_ref, kv_ref, dq_ref, g_ref, kt_ref, dk_ref, dv_ref = refs
        from_ref = None
    else:
        depth_ref, q_ref, do_ref, lt_ref, ot_ref, kv_ref, from_ref, dq_ref, g_ref, kt_ref, dk_ref, dv_ref = refs

    def work():
        kt_ref[...] = kv_ref[:, :dh].astype(F32).T.astype(BF16)
        dk_ref[...] = jnp.zeros_like(dk_ref)
        dv_ref[...] = jnp.zeros_like(dv_ref)
        for h in range(heads):
            hs = slice(h * dh, (h + 1) * dh)
            q, do = q_ref[:, hs], do_ref[:, hs]
            p = jnp.exp2(dot(kv_ref[:, :dh], q, 1, 1) * (scale * LOG2E) - lt_ref[h : h + 1, :])
            ds = (p * (dot(kv_ref[:, dh:], do, 1, 1) - ot_ref[h : h + 1, :])).astype(BF16)
            dk_ref[...] += dot(ds, q, 1, 0)
            dv_ref[...] += dot(p.astype(BF16), do, 1, 0)
            part = dot(kt_ref[...], ds, 1, 0)
            dq_ref[hs, :] = part if first else from_ref[hs, :] + part
        g_ref[:, :dh] = (dk_ref[...] * scale).astype(BF16)
        g_ref[:, dh:] = dv_ref[...].astype(BF16)

    if block == 0:
        work()
    else:
        pl.when(depth_ref[0] > block)(work)


def piece(depth, q, do, lt, ot, kv, dq, block):
    rows, width = q.shape
    heads = lt.shape[0]
    dh = width // heads
    keys = kv.shape[0]
    args = (depth, q, do, lt, ot, kv) + (() if dq is None else (dq,))
    return pl.pallas_call(
        functools.partial(piece_kernel, heads, dh, dh**-0.5, block, dq is None),
        in_specs=[SMEM] + [VMEM] * (len(args) - 1),
        out_specs=[VMEM] * 2,
        out_shape=[jax.ShapeDtypeStruct((width, rows), F32), jax.ShapeDtypeStruct((keys, 2 * dh), BF16)],
        scratch_shapes=[pltpu.VMEM((dh, keys), BF16), pltpu.VMEM((keys, dh), F32), pltpu.VMEM((keys, dh), F32)],
        input_output_aliases={} if dq is None else {6: 0},
        compiler_params=params(20),
        cost_estimate=cost(rows, keys, heads, dh),
        name="piece",
    )(*args)


def join_kernel(heads, dh, scale, own_ref, pool_ref, out_ref):
    for h in range(heads):
        hs = slice(h * dh, (h + 1) * dh)
        pool_term = (pool_ref[hs, :] * scale).astype(BF16).astype(F32)
        out_ref[:, hs] = (own_ref[hs, :] * scale + pool_term).T.astype(BF16)


def join(own_dq, pool_dq, heads):
    width, rows = own_dq.shape
    dh = width // heads
    return pl.pallas_call(
        functools.partial(join_kernel, heads, dh, dh**-0.5),
        in_specs=[VMEM] * 2,
        out_specs=VMEM,
        out_shape=jax.ShapeDtypeStruct((rows, width), BF16),
        compiler_params=params(8),
        name="join",
    )(own_dq, pool_dq)


def place_kernel(rows, table_ref, *refs):
    ins, out_ref, sem = refs[: len(PIECES)], refs[-2], refs[-1]
    copies = []
    for i, (block, first, size) in enumerate(PIECES):
        at = pl.multiple_of(table_ref[block] * rows + first, 128)
        copies.append(pltpu.make_async_copy(ins[i], out_ref.at[pl.ds(at, size), :], sem.at[i]))
    for c in copies:
        c.start()
    for c in copies:
        c.wait()


def place(table, parts, shape, rows):
    return pl.pallas_call(
        functools.partial(place_kernel, rows),
        in_specs=[SMEM] + [VMEM] * len(parts),
        out_specs=HBM,
        out_shape=jax.ShapeDtypeStruct(shape, BF16),
        scratch_shapes=[pltpu.SemaphoreType.DMA((len(PIECES),))],
        compiler_params=params(4),
        name="place",
    )(table, *parts)


def per_device(query, grad_output, log_total, offset, slice_keys, pool_keys, block_table):
    rows, heads = log_total.shape[1:]
    table = block_table[0]
    sections = lax.axis_size("section")
    half_axis = sections // 2
    group = sections // NSL
    depths = [NSL - 1 - layer // group % (NSL - 1) for layer in range(sections)]
    me = lax.axis_index("section")
    depth = (NSL - 1 - me // group % (NSL - 1)).astype(jnp.int32).reshape(1)

    def pairs(block):
        return [(layer, (layer + half_axis) % sections) for layer in range(sections) if depths[layer] > block]

    picked = pick(table, pool_keys[0], rows)
    arrived = []
    for i, (block, _, _) in enumerate(PIECES):
        arrived.append(lax.ppermute(picked[i], "section", [(p, layer) for layer, p in pairs(block)]))
    own_dq, slice_grad, lt, ot, q, do = own(query[0], grad_output[0], log_total[0].T, offset[0].T, slice_keys[0])
    dq = None
    parts = []
    for i, (block, _, _) in enumerate(PIECES):
        dq, g = piece(depth, q, do, lt, ot, arrived[i], dq, block)
        parts.append(lax.ppermute(g, "section", pairs(block)))
    query_grad = join(own_dq, dq, heads)
    pool_grad = place(table, parts, pool_keys.shape[1:], rows)
    return (query_grad[None], slice_grad[None], pool_grad[None])


def solution(mesh):
    spec = P("section", None, "kv")
    return jax.shard_map(
        per_device,
        mesh=mesh,
        in_specs=(spec, spec, spec, spec, spec, spec, P("section", None)),
        out_specs=(spec, spec, spec),
        check_vma=False,
    )
```

```python
import functools

import jax
import jax.numpy as jnp
from jax import lax
from jax.experimental import pallas as pl
from jax.experimental.pallas import tpu as pltpu
from jax.sharding import PartitionSpec as P


NSL = 4
LOG2E = 1.4426950408889634
F32 = jnp.float32
BF16 = jnp.bfloat16
VMEM = pl.BlockSpec(memory_space=pltpu.VMEM)
SMEM = pl.BlockSpec(memory_space=pltpu.SMEM)
HBM = pl.BlockSpec(memory_space=pltpu.HBM)
PIECES = ((0, 0, 512), (2, 0, 512), (1, 0, 512))


def dot(a, b, ca, cb):
    return lax.dot_general(a, b, (((ca,), (cb,)), ((), ())), preferred_element_type=F32)


def in_hbm(x):
    return pltpu.with_memory_space_constraint(x, pltpu.HBM)


def params(mib):
    return pltpu.CompilerParams(vmem_limit_bytes=mib << 20)


def cost(rows, keys, heads, dh):
    return pl.CostEstimate(
        flops=10 * rows * keys * heads * dh, bytes_accessed=1 << 20, transcendentals=rows * keys * heads
    )


def pick_kernel(rows, table_ref, pool_ref, *refs):
    outs, sem = refs[:-1], refs[-1]
    copies = []
    for i, (block, first, size) in enumerate(PIECES):
        at = pl.multiple_of(table_ref[block] * rows + first, 128)
        copies.append(pltpu.make_async_copy(pool_ref.at[pl.ds(at, size), :], outs[i], sem.at[i]))
    for c in copies:
        c.start()
    for c in copies:
        c.wait()


def pick(table, pool, rows):
    width = pool.shape[1]
    return pl.pallas_call(
        functools.partial(pick_kernel, rows),
        in_specs=[SMEM, HBM],
        out_specs=[VMEM] * len(PIECES),
        out_shape=[jax.ShapeDtypeStruct((size, width), pool.dtype) for _, _, size in PIECES],
        scratch_shapes=[pltpu.SemaphoreType.DMA((len(PIECES),))],
        compiler_params=params(4),
        name="pick",
    )(table, in_hbm(pool))


def prep_kernel(heads, dh, q_hbm, do_hbm, l_hbm, o_hbm, q_ref, do_ref, qt_ref, dot_ref, l_ref, o_ref, lraw_ref, oraw_ref, sem):
    rows = lraw_ref.shape[1]
    half = rows // 2
    small = [pltpu.make_async_copy(l_hbm, lraw_ref, sem.at[0]), pltpu.make_async_copy(o_hbm, oraw_ref, sem.at[1])]
    large = []
    for t in range(2):
        for h in range(heads):
            at = (t * heads + h) * half
            for a, b in ((q_hbm, q_ref), (do_hbm, do_ref)):
                large.append(
                    pltpu.make_async_copy(
                        a.at[pl.ds(t * half, half), pl.ds(h * dh, dh)], b.at[pl.ds(at, half), :], sem.at[2 + len(large)]
                    )
                )
    for c in small + large:
        c.start()
    for c in small:
        c.wait()
    lcol = (lraw_ref[...].astype(F32) * LOG2E).T
    ocol = oraw_ref[...].astype(F32).T
    for t in range(2):
        for h in range(heads):
            part = slice((t * heads + h) * half, (t * heads + h + 1) * half)
            l_ref[part, :] = jnp.broadcast_to(lcol[t * half : (t + 1) * half, h : h + 1], (half, dh))
            o_ref[part, :] = jnp.broadcast_to(ocol[t * half : (t + 1) * half, h : h + 1], (half, dh))
    for i in range(2 * heads):
        part = slice(i * half, (i + 1) * half)
        large[2 * i].wait()
        qt_ref[:, part] = q_ref[part, :].T
        large[2 * i + 1].wait()
        dot_ref[:, part] = do_ref[part, :].T


def prep(q, do, totals, offsets):
    rows, width = q.shape
    heads = totals.shape[0]
    dh = width // heads
    many = heads * rows
    return pl.pallas_call(
        functools.partial(prep_kernel, heads, dh),
        in_specs=[HBM] * 4,
        out_specs=[VMEM] * 6,
        out_shape=[
            jax.ShapeDtypeStruct((many, dh), BF16),
            jax.ShapeDtypeStruct((many, dh), BF16),
            jax.ShapeDtypeStruct((dh, many), BF16),
            jax.ShapeDtypeStruct((dh, many), BF16),
            jax.ShapeDtypeStruct((many, dh), F32),
            jax.ShapeDtypeStruct((many, dh), F32),
        ],
        scratch_shapes=[
            pltpu.VMEM((heads, rows), BF16),
            pltpu.VMEM((heads, rows), BF16),
            pltpu.SemaphoreType.DMA((2 + 4 * heads,)),
        ],
        compiler_params=params(16),
        cost_estimate=pl.CostEstimate(flops=1000, bytes_accessed=4 << 20, transcendentals=0),
        name="prep",
    )(*(in_hbm(x) for x in (q, do, totals, offsets)))


def own_kernel(heads, scale, q_ref, do_ref, qt_ref, dot_ref, l_ref, o_ref, kv_ref, pool_ref, out_ref, g_ref, dk_ref, dv_ref):
    many, dh = q_ref.shape
    half = many // heads // 2
    step = many // 4
    key_ids = lax.broadcasted_iota(jnp.int32, (step, half), 1)
    row_ids = lax.rem(lax.broadcasted_iota(jnp.int32, (step, half), 0), half)
    visible = key_ids <= row_ids
    k, v = kv_ref[:, :dh], kv_ref[:, dh:]
    for c in (2, 3, 0, 1):
        t = c // 2
        rs = slice(c * step, (c + 1) * step)
        keys = (t + 1) * half
        over = keys // dh
        s = dot(q_ref[rs, :], k[:keys], 1, 1)
        dp = dot(do_ref[rs, :], v[:keys], 1, 1)
        p = jnp.exp2(s * (scale * LOG2E) - jnp.concatenate([l_ref[rs, :]] * over, axis=1))
        last = jnp.where(visible, p[:, keys - half :], 0.0)
        p = last if t == 0 else jnp.concatenate([p[:, :half], last], axis=1)
        ds = (p * (dp - jnp.concatenate([o_ref[rs, :]] * over, axis=1))).astype(BF16)
        dq = dot(ds, k[:keys], 1, 0)
        for i in range(heads // 2):
            h = (c % 2) * (heads // 2) + i
            pool_term = (pool_ref[c * step + i * half : c * step + (i + 1) * half, :] * scale).astype(BF16).astype(F32)
            total = dq[i * half : (i + 1) * half, :] * scale + pool_term
            out_ref[t * half : (t + 1) * half, h * dh : (h + 1) * dh] = total.astype(BF16)
        dk = dot(qt_ref[:, rs], ds, 1, 0)
        dv = dot(dot_ref[:, rs], p.astype(BF16), 1, 0)
        if c == 2:
            dk_ref[...] = dk
            dv_ref[...] = dv
        else:
            dk_ref[:, :keys] += dk
            dv_ref[:, :keys] += dv
    g_ref[:, :dh] = (dk_ref[...].T * scale).astype(BF16)
    g_ref[:, dh:] = dv_ref[...].T.astype(BF16)


def own(rows_of, kv, pool_dq):
    many, dh = pool_dq.shape
    rows = kv.shape[0]
    heads = many // rows
    return pl.pallas_call(
        functools.partial(own_kernel, heads, dh**-0.5),
        in_specs=[VMEM] * 8,
        out_specs=[VMEM] * 2,
        out_shape=[jax.ShapeDtypeStruct((rows, heads * dh), BF16), jax.ShapeDtypeStruct((rows, 2 * dh), BF16)],
        scratch_shapes=[pltpu.VMEM((dh, rows), F32), pltpu.VMEM((dh, rows), F32)],
        compiler_params=params(24),
        cost_estimate=cost(many, rows * 3 // 4, 1, dh),
        name="own",
    )(*rows_of, kv, pool_dq)


def piece_kernel(step, scale, block, first, *refs):
    if first:
        depth_ref, q_ref, do_ref, qt_ref, dot_ref, l_ref, o_ref, kv_ref, dq_ref, g_ref, dk_ref, dv_ref = refs
    else:
        depth_ref, q_ref, do_ref, qt_ref, dot_ref, l_ref, o_ref, kv_ref, from_ref, dq_ref, g_ref, dk_ref, dv_ref = refs
    many, dh = q_ref.shape
    over = kv_ref.shape[0] // dh

    def work():
        k, v = kv_ref[:, :dh], kv_ref[:, dh:]
        for c in range(many // step):
            rs = slice(c * step, (c + 1) * step)
            s = dot(q_ref[rs, :], k, 1, 1)
            dp = dot(do_ref[rs, :], v, 1, 1)
            p = jnp.exp2(s * (scale * LOG2E) - jnp.concatenate([l_ref[rs, :]] * over, axis=1))
            ds = (p * (dp - jnp.concatenate([o_ref[rs, :]] * over, axis=1))).astype(BF16)
            part = dot(ds, k, 1, 0)
            dq_ref[rs, :] = part if first else from_ref[rs, :] + part
            dk = dot(qt_ref[:, rs], ds, 1, 0)
            dv = dot(dot_ref[:, rs], p.astype(BF16), 1, 0)
            if c == 0:
                dk_ref[...] = dk
                dv_ref[...] = dv
            else:
                dk_ref[...] += dk
                dv_ref[...] += dv
        g_ref[:, :dh] = (dk_ref[...].T * scale).astype(BF16)
        g_ref[:, dh:] = dv_ref[...].T.astype(BF16)

    if block == 0:
        work()
        return
    pl.when(depth_ref[0] > block)(work)

    @pl.when(depth_ref[0] <= block)
    def _():
        g_ref[...] = jnp.zeros_like(g_ref)


def piece(depth, rows_of, kv, dq, block):
    many, dh = rows_of[0].shape
    keys = kv.shape[0]
    args = (depth, *rows_of, kv) + (() if dq is None else (dq,))
    return pl.pallas_call(
        functools.partial(piece_kernel, many // 4, dh**-0.5, block, dq is None),
        in_specs=[SMEM] + [VMEM] * (len(args) - 1),
        out_specs=[VMEM] * 2,
        out_shape=[jax.ShapeDtypeStruct((many, dh), F32), jax.ShapeDtypeStruct((keys, 2 * dh), BF16)],
        scratch_shapes=[pltpu.VMEM((dh, keys), F32), pltpu.VMEM((dh, keys), F32)],
        input_output_aliases={} if dq is None else {8: 0},
        compiler_params=params(24),
        cost_estimate=cost(many, keys, 1, dh),
        name="piece",
    )(*args)


def place_kernel(rows, table_ref, *refs):
    ins, out_ref, sem = refs[: len(PIECES)], refs[-2], refs[-1]
    copies = []
    for i, (block, first, size) in enumerate(PIECES):
        at = pl.multiple_of(table_ref[block] * rows + first, 128)
        copies.append(pltpu.make_async_copy(ins[i], out_ref.at[pl.ds(at, size), :], sem.at[i]))
    for c in copies:
        c.start()
    for c in copies:
        c.wait()


def place(table, parts, shape, rows):
    return pl.pallas_call(
        functools.partial(place_kernel, rows),
        in_specs=[SMEM] + [VMEM] * len(parts),
        out_specs=HBM,
        out_shape=jax.ShapeDtypeStruct(shape, BF16),
        scratch_shapes=[pltpu.SemaphoreType.DMA((len(PIECES),))],
        compiler_params=params(4),
        name="place",
    )(table, *parts)


def per_device(query, grad_output, log_total, offset, slice_keys, pool_keys, block_table):
    rows, _ = log_total.shape[1:]
    table = block_table[0]
    sections = lax.axis_size("section")
    half_axis = sections // 2
    group = sections // NSL
    depths = [NSL - 1 - layer // group % (NSL - 1) for layer in range(sections)]
    me = lax.axis_index("section")
    depth = (NSL - 1 - me // group % (NSL - 1)).astype(jnp.int32).reshape(1)

    swap = [(layer, (layer + half_axis) % sections) for layer in range(sections)]
    deep = [(p, layer) for layer, p in swap if depths[layer] == NSL - 1]

    picked = pick(table, pool_keys[0], rows)
    arrived = []
    for i, (block, _, _) in enumerate(PIECES):
        arrived.append(lax.ppermute(picked[i], "section", deep if block == NSL - 2 else swap))
    rows_of = prep(query[0], grad_output[0], log_total[0].T, offset[0].T)
    dq = None
    parts = []
    for i, (block, _, _) in enumerate(PIECES):
        dq, g = piece(depth, rows_of, arrived[i], dq, block)
        parts.append(lax.ppermute(g, "section", swap))
    query_grad, slice_grad = own(rows_of, slice_keys[0], dq)
    pool_grad = place(table, parts, pool_keys.shape[1:], rows)
    return (query_grad[None], slice_grad[None], pool_grad[None])


def solution(mesh):
    spec = P("section", None, "kv")
    return jax.shard_map(
        per_device,
        mesh=mesh,
        in_specs=(spec, spec, spec, spec, spec, spec, P("section", None)),
        out_specs=(spec, spec, spec),
        check_vma=False,
    )
```

```python
import functools

import jax
import jax.numpy as jnp
from jax import lax
from jax.experimental import pallas as pl
from jax.experimental.pallas import tpu as pltpu
from jax.sharding import PartitionSpec as P


NSL = 4
LOG2E = 1.4426950408889634
F32 = jnp.float32
BF16 = jnp.bfloat16
VMEM = pl.BlockSpec(memory_space=pltpu.VMEM)
SMEM = pl.BlockSpec(memory_space=pltpu.SMEM)
HBM = pl.BlockSpec(memory_space=pltpu.HBM)
BLOCKS = (0, 2, 1)
PIECES = ((0, 0, 512), (2, 0, 512), (1, 0, 256), (1, 256, 256))


def dot(a, b, ca, cb):
    return lax.dot_general(a, b, (((ca,), (cb,)), ((), ())), preferred_element_type=F32)


def in_hbm(x):
    return pltpu.with_memory_space_constraint(x, pltpu.HBM)


def params(mib):
    return pltpu.CompilerParams(vmem_limit_bytes=mib << 20)


def cost(rows, keys, heads, dh):
    return pl.CostEstimate(
        flops=10 * rows * keys * heads * dh, bytes_accessed=1 << 20, transcendentals=rows * keys * heads
    )


def pick_kernel(rows, table_hbm, pool_ref, *refs):
    outs, table_ref, sem = refs[:-2], refs[-2], refs[-1]
    first = pltpu.make_async_copy(table_hbm, table_ref, sem.at[len(BLOCKS)])
    first.start()
    first.wait()
    copies = []
    for i, block in enumerate(BLOCKS):
        at = pl.multiple_of(table_ref[0, block] * rows, 128)
        copies.append(pltpu.make_async_copy(pool_ref.at[pl.ds(at, rows), :], outs[i], sem.at[i]))
    for c in copies:
        c.start()
    for c in copies:
        c.wait()


def pick(table, pool, rows):
    width = pool.shape[1]
    return pl.pallas_call(
        functools.partial(pick_kernel, rows),
        in_specs=[HBM, HBM],
        out_specs=[VMEM] * len(BLOCKS),
        out_shape=[jax.ShapeDtypeStruct((rows, width), pool.dtype)] * len(BLOCKS),
        scratch_shapes=[pltpu.SMEM(table.shape, jnp.int32), pltpu.SemaphoreType.DMA((len(BLOCKS) + 1,))],
        compiler_params=params(4),
        name="pick",
    )(in_hbm(table), in_hbm(pool))


def stretch(ref, c, heads):
    half, dh = ref.shape[0] // 2, ref.shape[1] // heads
    t, h0 = c // 2, (c % 2) * (heads // 2)
    rs = slice(t * half, (t + 1) * half)
    return jnp.concatenate([ref[rs, h * dh : (h + 1) * dh] for h in range(h0, h0 + heads // 2)], axis=0)


def prep_kernel(heads, dh, q_hbm, do_hbm, l_hbm, o_hbm, q_ref, do_ref, qt_ref, dot_ref, l_ref, o_ref, lraw_ref, oraw_ref, sem):
    rows = lraw_ref.shape[1]
    half = rows // 2
    small = [pltpu.make_async_copy(l_hbm, lraw_ref, sem.at[0]), pltpu.make_async_copy(o_hbm, oraw_ref, sem.at[1])]
    large = []
    for t in range(2):
        for a, b in ((q_hbm, q_ref), (do_hbm, do_ref)):
            rs = pl.ds(t * half, half)
            large.append(pltpu.make_async_copy(a.at[rs, :], b.at[rs, :], sem.at[2 + len(large)]))
    for c in small + large:
        c.start()
    for c in small:
        c.wait()
    lcol = (lraw_ref[...].astype(F32) * LOG2E).T
    ocol = oraw_ref[...].astype(F32).T
    for t in range(2):
        rs = slice(t * half, (t + 1) * half)
        for h in range(heads):
            part = slice((t * heads + h) * half, (t * heads + h + 1) * half)
            l_ref[part, :] = jnp.broadcast_to(lcol[rs, h : h + 1], (half, dh))
            o_ref[part, :] = jnp.broadcast_to(ocol[rs, h : h + 1], (half, dh))
    for t in range(2):
        rs = slice(t * half, (t + 1) * half)
        for i, (a, b) in enumerate(((q_ref, qt_ref), (do_ref, dot_ref))):
            large[2 * t + i].wait()
            for h in range(heads):
                part = slice((t * heads + h) * half, (t * heads + h + 1) * half)
                b[:, part] = a[rs, h * dh : (h + 1) * dh].T


def prep(q, do, totals, offsets):
    rows, width = q.shape
    heads = totals.shape[0]
    dh = width // heads
    many = heads * rows
    return pl.pallas_call(
        functools.partial(prep_kernel, heads, dh),
        in_specs=[HBM] * 4,
        out_specs=[VMEM] * 6,
        out_shape=[
            jax.ShapeDtypeStruct((rows, width), BF16),
            jax.ShapeDtypeStruct((rows, width), BF16),
            jax.ShapeDtypeStruct((dh, many), BF16),
            jax.ShapeDtypeStruct((dh, many), BF16),
            jax.ShapeDtypeStruct((many, dh), F32),
            jax.ShapeDtypeStruct((many, dh), F32),
        ],
        scratch_shapes=[
            pltpu.VMEM((heads, rows), BF16),
            pltpu.VMEM((heads, rows), BF16),
            pltpu.SemaphoreType.DMA((6,)),
        ],
        compiler_params=params(16),
        cost_estimate=pl.CostEstimate(flops=1000, bytes_accessed=4 << 20, transcendentals=0),
        name="prep",
    )(*(in_hbm(x) for x in (q, do, totals, offsets)))


def own_kernel(heads, scale, q_ref, do_ref, qt_ref, dot_ref, l_ref, o_ref, kv_ref, pool_ref, out_hbm, g_hbm, out_ref, g_ref, dk_ref, dv_ref, sem):
    many, dh = l_ref.shape
    half = many // heads // 2
    step = many // 4
    key_ids = lax.broadcasted_iota(jnp.int32, (step, half), 1)
    row_ids = lax.rem(lax.broadcasted_iota(jnp.int32, (step, half), 0), half)
    visible = key_ids <= row_ids
    k, v = kv_ref[:, :dh], kv_ref[:, dh:]
    copies = []
    for c in (2, 3, 0, 1):
        t = c // 2
        rs = slice(c * step, (c + 1) * step)
        keys = (t + 1) * half
        over = keys // dh
        s = dot(stretch(q_ref, c, heads), k[:keys], 1, 1)
        dp = dot(stretch(do_ref, c, heads), v[:keys], 1, 1)
        p = jnp.exp2(s * (scale * LOG2E) - jnp.concatenate([l_ref[rs, :]] * over, axis=1))
        last = jnp.where(visible, p[:, keys - half :], 0.0)
        p = last if t == 0 else jnp.concatenate([p[:, :half], last], axis=1)
        ds = (p * (dp - jnp.concatenate([o_ref[rs, :]] * over, axis=1))).astype(BF16)
        dq = dot(ds, k[:keys], 1, 0)
        for i in range(heads // 2):
            h = (c % 2) * (heads // 2) + i
            pool_term = (pool_ref[c * step + i * half : c * step + (i + 1) * half, :] * scale).astype(BF16).astype(F32)
            total = dq[i * half : (i + 1) * half, :] * scale + pool_term
            out_ref[t * half : (t + 1) * half, h * dh : (h + 1) * dh] = total.astype(BF16)
        wide = heads // 2 * dh
        place_of = (pl.ds(t * half, half), pl.ds(c % 2 * wide, wide))
        copies.append(pltpu.make_async_copy(out_ref.at[place_of], out_hbm.at[place_of], sem.at[c]))
        copies[-1].start()
        dk = dot(qt_ref[:, rs], ds, 1, 0)
        dv = dot(dot_ref[:, rs], p.astype(BF16), 1, 0)
        if c == 2:
            dk_ref[...] = dk
            dv_ref[...] = dv
        else:
            dk_ref[:, :keys] += dk
            dv_ref[:, :keys] += dv
    g_ref[:, :dh] = (dk_ref[...].T * scale).astype(BF16)
    g_ref[:, dh:] = dv_ref[...].T.astype(BF16)
    copies.append(pltpu.make_async_copy(g_ref, g_hbm, sem.at[4]))
    copies[-1].start()
    for copy in copies:
        copy.wait()


def own(rows_of, kv, pool_dq):
    many, dh = pool_dq.shape
    rows = kv.shape[0]
    heads = many // rows
    return pl.pallas_call(
        functools.partial(own_kernel, heads, dh**-0.5),
        in_specs=[VMEM] * 8,
        out_specs=[HBM] * 2,
        out_shape=[jax.ShapeDtypeStruct((rows, heads * dh), BF16), jax.ShapeDtypeStruct((rows, 2 * dh), BF16)],
        scratch_shapes=[
            pltpu.VMEM((rows, heads * dh), BF16),
            pltpu.VMEM((rows, 2 * dh), BF16),
            pltpu.VMEM((dh, rows), F32),
            pltpu.VMEM((dh, rows), F32),
            pltpu.SemaphoreType.DMA((5,)),
        ],
        compiler_params=params(24),
        cost_estimate=cost(many, rows * 3 // 4, 1, dh),
        name="own",
    )(*rows_of, kv, pool_dq)


def piece_kernel(heads, scale, block, start, first, *refs):
    depth_ref, q_ref, do_ref, qt_ref, dot_ref, l_ref, o_ref, kv_ref = refs[:8]
    split = block == 1
    from_ref = None if first else refs[8]
    outs = refs[8 + (not first) + (split and start > 0) :]
    dq_ref, g_ref = outs[:2]
    next_ref = outs[2] if split and start == 0 else None
    dk_ref, dv_ref = outs[-2:]
    many, dh = l_ref.shape
    step = many // 4
    size = g_ref.shape[0]

    def work(keys, to):
        k, v = kv_ref[start : start + keys, :dh], kv_ref[start : start + keys, dh:]
        over = keys // dh
        for c in range(4):
            rs = slice(c * step, (c + 1) * step)
            s = dot(stretch(q_ref, c, heads), k, 1, 1)
            dp = dot(stretch(do_ref, c, heads), v, 1, 1)
            p = jnp.exp2(s * (scale * LOG2E) - jnp.concatenate([l_ref[rs, :]] * over, axis=1))
            ds = (p * (dp - jnp.concatenate([o_ref[rs, :]] * over, axis=1))).astype(BF16)
            part = dot(ds, k, 1, 0)
            dq_ref[rs, :] = part if first else from_ref[rs, :] + part
            dk = dot(qt_ref[:, rs], ds, 1, 0)
            dv = dot(dot_ref[:, rs], p.astype(BF16), 1, 0)
            if c == 0:
                dk_ref[:, :keys] = dk
                dv_ref[:, :keys] = dv
            else:
                dk_ref[:, :keys] += dk
                dv_ref[:, :keys] += dv
        for i, ref in enumerate(to):
            ks = slice(i * size, (i + 1) * size)
            ref[:, :dh] = (dk_ref[:, ks].T * scale).astype(BF16)
            ref[:, dh:] = dv_ref[:, ks].T.astype(BF16)

    if block == 0:
        work(size, (g_ref,))
        return

    @pl.when(depth_ref[0] == NSL - 1)
    def _():
        work(size, (g_ref,))

    if split and start > 0:
        return
    unused = depth_ref[0] <= block
    if split:

        @pl.when(depth_ref[0] == NSL - 2)
        def _():
            work(2 * size, (g_ref, next_ref))

    @pl.when(unused)
    def _():
        g_ref[...] = jnp.zeros_like(g_ref)
        if split:
            next_ref[...] = jnp.zeros_like(next_ref)


def piece(depth, rows_of, kv, dq, held, block, start, size):
    many, dh = rows_of[-1].shape
    split = block == 1
    args = (depth, *rows_of, kv) + (() if dq is None else (dq,)) + (() if held is None else (held,))
    gave = jax.ShapeDtypeStruct((size, 2 * dh), BF16)
    keys = 2 * size if split and start == 0 else size
    return pl.pallas_call(
        functools.partial(piece_kernel, many // kv.shape[0], dh**-0.5, block, start, dq is None),
        in_specs=[SMEM] + [VMEM] * (len(args) - 1),
        out_specs=[VMEM] * (3 if split and start == 0 else 2),
        out_shape=[jax.ShapeDtypeStruct((many, dh), F32), gave] + ([gave] if split and start == 0 else []),
        scratch_shapes=[pltpu.VMEM((dh, keys), F32), pltpu.VMEM((dh, keys), F32)],
        input_output_aliases=({} if dq is None else {8: 0}) | ({} if held is None else {9: 1}),
        compiler_params=params(24),
        cost_estimate=cost(many, size, 1, dh),
        name="piece",
    )(*args)


def place_kernel(rows, table_ref, *refs):
    ins, out_ref, sem = refs[: len(PIECES)], refs[-2], refs[-1]
    copies = []
    for i, (block, first, size) in enumerate(PIECES):
        at = pl.multiple_of(table_ref[block] * rows + first, 128)
        copies.append(pltpu.make_async_copy(ins[i], out_ref.at[pl.ds(at, size), :], sem.at[i]))
    for c in copies:
        c.start()
    for c in copies:
        c.wait()


def place(table, parts, shape, rows):
    return pl.pallas_call(
        functools.partial(place_kernel, rows),
        in_specs=[SMEM] + [VMEM] * len(parts),
        out_specs=HBM,
        out_shape=jax.ShapeDtypeStruct(shape, BF16),
        scratch_shapes=[pltpu.SemaphoreType.DMA((len(PIECES),))],
        compiler_params=params(4),
        name="place",
    )(table, *parts)


def per_device(query, grad_output, log_total, offset, slice_keys, pool_keys, block_table):
    rows, _ = log_total.shape[1:]
    table = block_table[0]
    sections = lax.axis_size("section")
    half_axis = sections // 2
    group = sections // NSL
    depths = [NSL - 1 - layer // group % (NSL - 1) for layer in range(sections)]
    me = lax.axis_index("section")
    depth = (NSL - 1 - me // group % (NSL - 1)).astype(jnp.int32).reshape(1)

    swap = [(layer, (layer + half_axis) % sections) for layer in range(sections)]
    home = [(layer, p) for layer, p in swap if depths[layer] == NSL - 1]
    deep = [(p, layer) for layer, p in swap if depths[layer] == NSL - 1]

    picked = pick(block_table, pool_keys[0], rows)
    arrived = {}
    for i, block in enumerate(BLOCKS):
        arrived[block] = lax.ppermute(picked[i], "section", deep if block == NSL - 2 else swap)
    rows_of = prep(query[0], grad_output[0], log_total[0].T, offset[0].T)
    dq = held = None
    parts = []
    for block, start, size in PIECES:
        dq, g, *rest = piece(depth, rows_of, arrived[block], dq, held, block, start, size)
        held = rest[0] if rest else None
        parts.append(lax.ppermute(g, "section", home if block == NSL - 2 else swap))
    query_grad, slice_grad = own(rows_of, slice_keys[0], dq)
    pool_grad = place(table, parts, pool_keys.shape[1:], rows)
    return (query_grad[None], slice_grad[None], pool_grad[None])


def solution(mesh):
    spec = P("section", None, "kv")
    return jax.shard_map(
        per_device,
        mesh=mesh,
        in_specs=(spec, spec, spec, spec, spec, spec, P("section", None)),
        out_specs=(spec, spec, spec),
        check_vma=False,
    )
```

```python
import functools

import jax
import jax.numpy as jnp
from jax import lax
from jax.experimental import pallas as pl
from jax.experimental.pallas import tpu as pltpu
from jax.sharding import PartitionSpec as P


NSL = 4
LOG2E = 1.4426950408889634
F32 = jnp.float32
BF16 = jnp.bfloat16
VMEM = pl.BlockSpec(memory_space=pltpu.VMEM)
SMEM = pl.BlockSpec(memory_space=pltpu.SMEM)
HBM = pl.BlockSpec(memory_space=pltpu.HBM)
BLOCKS = (0, 2, 1)
PIECES = ((0, 0, 512), (2, 0, 512), (1, 0, 256), (1, 256, 256))


def dot(a, b, ca, cb):
    return lax.dot_general(a, b, (((ca,), (cb,)), ((), ())), preferred_element_type=F32)


def in_hbm(x):
    return pltpu.with_memory_space_constraint(x, pltpu.HBM)


def params(mib):
    return pltpu.CompilerParams(vmem_limit_bytes=mib << 20)


def cost(rows, keys, heads, dh):
    return pl.CostEstimate(
        flops=10 * rows * keys * heads * dh, bytes_accessed=1 << 20, transcendentals=rows * keys * heads
    )


def pick_kernel(rows, table_hbm, pool_ref, *refs):
    outs, table_ref, sem = refs[:-2], refs[-2], refs[-1]
    first = pltpu.make_async_copy(table_hbm, table_ref, sem.at[len(BLOCKS)])
    first.start()
    first.wait()
    copies = []
    for i, block in enumerate(BLOCKS):
        at = pl.multiple_of(table_ref[0, block] * rows, 128)
        copies.append(pltpu.make_async_copy(pool_ref.at[pl.ds(at, rows), :], outs[i], sem.at[i]))
    for c in copies:
        c.start()
    for c in copies:
        c.wait()


def pick(table, pool, rows):
    width = pool.shape[1]
    return pl.pallas_call(
        functools.partial(pick_kernel, rows),
        in_specs=[HBM, HBM],
        out_specs=[VMEM] * len(BLOCKS),
        out_shape=[jax.ShapeDtypeStruct((rows, width), pool.dtype)] * len(BLOCKS),
        scratch_shapes=[pltpu.SMEM(table.shape, jnp.int32), pltpu.SemaphoreType.DMA((len(BLOCKS) + 1,))],
        compiler_params=params(4),
        name="pick",
    )(in_hbm(table), in_hbm(pool))


def stretch(ref, c, heads):
    half, dh = ref.shape[0] // 2, ref.shape[1] // heads
    t, h0 = c // 2, (c % 2) * (heads // 2)
    rs = slice(t * half, (t + 1) * half)
    return jnp.concatenate([ref[rs, h * dh : (h + 1) * dh] for h in range(h0, h0 + heads // 2)], axis=0)


def prep_kernel(heads, dh, q_hbm, do_hbm, l_hbm, o_hbm, q_ref, do_ref, qt_ref, dot_ref, l_ref, o_ref, lraw_ref, oraw_ref, sem):
    rows = lraw_ref.shape[1]
    half = rows // 2
    small = [pltpu.make_async_copy(l_hbm, lraw_ref, sem.at[0]), pltpu.make_async_copy(o_hbm, oraw_ref, sem.at[1])]
    large = []
    for t in range(2):
        for a, b in ((q_hbm, q_ref), (do_hbm, do_ref)):
            rs = pl.ds(t * half, half)
            large.append(pltpu.make_async_copy(a.at[rs, :], b.at[rs, :], sem.at[2 + len(large)]))
    for c in small + large:
        c.start()
    for c in small:
        c.wait()
    lcol = (lraw_ref[...].astype(F32) * LOG2E).T
    ocol = oraw_ref[...].astype(F32).T
    for t in range(2):
        rs = slice(t * half, (t + 1) * half)
        for h in range(heads):
            part = slice((t * heads + h) * half, (t * heads + h + 1) * half)
            l_ref[part, :] = jnp.broadcast_to(lcol[rs, h : h + 1], (half, dh))
            o_ref[part, :] = jnp.broadcast_to(ocol[rs, h : h + 1], (half, dh))
    for t in range(2):
        rs = slice(t * half, (t + 1) * half)
        for i, (a, b) in enumerate(((q_ref, qt_ref), (do_ref, dot_ref))):
            large[2 * t + i].wait()
            for h in range(heads):
                part = slice((t * heads + h) * half, (t * heads + h + 1) * half)
                b[:, part] = a[rs, h * dh : (h + 1) * dh].T


def prep(q, do, totals, offsets):
    rows, width = q.shape
    heads = totals.shape[0]
    dh = width // heads
    many = heads * rows
    return pl.pallas_call(
        functools.partial(prep_kernel, heads, dh),
        in_specs=[HBM] * 4,
        out_specs=[VMEM] * 6,
        out_shape=[
            jax.ShapeDtypeStruct((rows, width), BF16),
            jax.ShapeDtypeStruct((rows, width), BF16),
            jax.ShapeDtypeStruct((dh, many), BF16),
            jax.ShapeDtypeStruct((dh, many), BF16),
            jax.ShapeDtypeStruct((many, dh), F32),
            jax.ShapeDtypeStruct((many, dh), F32),
        ],
        scratch_shapes=[
            pltpu.VMEM((heads, rows), BF16),
            pltpu.VMEM((heads, rows), BF16),
            pltpu.SemaphoreType.DMA((6,)),
        ],
        compiler_params=params(16),
        cost_estimate=pl.CostEstimate(flops=1000, bytes_accessed=4 << 20, transcendentals=0),
        name="prep",
    )(*(in_hbm(x) for x in (q, do, totals, offsets)))


def own_kernel(heads, scale, q_ref, do_ref, qt_ref, dot_ref, l_ref, o_ref, kv_ref, pool_ref, out_hbm, g_hbm, out_ref, g_ref, dk_ref, dv_ref, sem):
    many, dh = l_ref.shape
    half = many // heads // 2
    step = many // 4
    key_ids = lax.broadcasted_iota(jnp.int32, (step, half), 1)
    row_ids = lax.rem(lax.broadcasted_iota(jnp.int32, (step, half), 0), half)
    visible = key_ids <= row_ids
    k, v = kv_ref[:, :dh], kv_ref[:, dh:]
    copies = []
    for c in (2, 3, 0, 1):
        t = c // 2
        rs = slice(c * step, (c + 1) * step)
        keys = (t + 1) * half
        over = keys // dh
        s = dot(stretch(q_ref, c, heads), k[:keys], 1, 1)
        dp = dot(stretch(do_ref, c, heads), v[:keys], 1, 1)
        p = jnp.exp2(s * (scale * LOG2E) - jnp.concatenate([l_ref[rs, :]] * over, axis=1))
        last = jnp.where(visible, p[:, keys - half :], 0.0)
        p = last if t == 0 else jnp.concatenate([p[:, :half], last], axis=1)
        ds = (p * (dp - jnp.concatenate([o_ref[rs, :]] * over, axis=1))).astype(BF16)
        dq = dot(ds, k[:keys], 1, 0)
        for i in range(heads // 2):
            h = (c % 2) * (heads // 2) + i
            pool_term = (pool_ref[c * step + i * half : c * step + (i + 1) * half, :] * scale).astype(BF16).astype(F32)
            total = dq[i * half : (i + 1) * half, :] * scale + pool_term
            out_ref[t * half : (t + 1) * half, h * dh : (h + 1) * dh] = total.astype(BF16)
        wide = heads // 2 * dh
        place_of = (pl.ds(t * half, half), pl.ds(c % 2 * wide, wide))
        copies.append(pltpu.make_async_copy(out_ref.at[place_of], out_hbm.at[place_of], sem.at[c]))
        copies[-1].start()
        dk = dot(qt_ref[:, rs], ds, 1, 0)
        dv = dot(dot_ref[:, rs], p.astype(BF16), 1, 0)
        if c == 2:
            dk_ref[...] = dk
            dv_ref[...] = dv
        else:
            dk_ref[:, :keys] += dk
            dv_ref[:, :keys] += dv
    g_ref[:, :dh] = (dk_ref[...].T * scale).astype(BF16)
    g_ref[:, dh:] = dv_ref[...].T.astype(BF16)
    copies.append(pltpu.make_async_copy(g_ref, g_hbm, sem.at[4]))
    copies[-1].start()
    for copy in copies:
        copy.wait()


def own(rows_of, kv, pool_dq):
    many, dh = pool_dq.shape
    rows = kv.shape[0]
    heads = many // rows
    return pl.pallas_call(
        functools.partial(own_kernel, heads, dh**-0.5),
        in_specs=[VMEM] * 8,
        out_specs=[HBM] * 2,
        out_shape=[jax.ShapeDtypeStruct((rows, heads * dh), BF16), jax.ShapeDtypeStruct((rows, 2 * dh), BF16)],
        scratch_shapes=[
            pltpu.VMEM((rows, heads * dh), BF16),
            pltpu.VMEM((rows, 2 * dh), BF16),
            pltpu.VMEM((dh, rows), F32),
            pltpu.VMEM((dh, rows), F32),
            pltpu.SemaphoreType.DMA((5,)),
        ],
        compiler_params=params(24),
        cost_estimate=cost(many, rows * 3 // 4, 1, dh),
        name="own",
    )(*rows_of, kv, pool_dq)


def piece_kernel(heads, scale, block, start, first, *refs):
    depth_ref, q_ref, do_ref, qt_ref, dot_ref, l_ref, o_ref, kv_ref = refs[:8]
    split = block == 1
    from_ref = None if first else refs[8]
    outs = refs[8 + (not first) + split :]
    other_ref = refs[9] if split and start == 0 else None
    dq_ref, g_ref = outs[:2]
    next_ref, both_ref = (outs[2], outs[3]) if split and start == 0 else (None, None)
    dk_ref, dv_ref = outs[-2:]
    many, dh = l_ref.shape
    step = many // 4
    size = g_ref.shape[0]

    def work(keys, to, kv=kv_ref):
        k, v = kv[start : start + keys, :dh], kv[start : start + keys, dh:]
        over = keys // dh
        for c in range(4):
            rs = slice(c * step, (c + 1) * step)
            s = dot(stretch(q_ref, c, heads), k, 1, 1)
            dp = dot(stretch(do_ref, c, heads), v, 1, 1)
            p = jnp.exp2(s * (scale * LOG2E) - jnp.concatenate([l_ref[rs, :]] * over, axis=1))
            ds = (p * (dp - jnp.concatenate([o_ref[rs, :]] * over, axis=1))).astype(BF16)
            part = dot(ds, k, 1, 0)
            dq_ref[rs, :] = part if first else from_ref[rs, :] + part
            dk = dot(qt_ref[:, rs], ds, 1, 0)
            dv = dot(dot_ref[:, rs], p.astype(BF16), 1, 0)
            if c == 0:
                dk_ref[:, :keys] = dk
                dv_ref[:, :keys] = dv
            else:
                dk_ref[:, :keys] += dk
                dv_ref[:, :keys] += dv
        for i, ref in enumerate(to):
            ks = slice(i * size, (i + 1) * size)
            ref[:, :dh] = (dk_ref[:, ks].T * scale).astype(BF16)
            ref[:, dh:] = dv_ref[:, ks].T.astype(BF16)

    if block == 0:

        @pl.when(depth_ref[0] > 1)
        def _():
            work(size, (g_ref,))

        @pl.when(depth_ref[0] <= 1)
        def _():
            dq_ref[...] = jnp.zeros_like(dq_ref)
            g_ref[...] = jnp.zeros_like(g_ref)

        return

    @pl.when(depth_ref[0] == NSL - 1)
    def _():
        work(size, (g_ref,))

    if split and start > 0:
        return

    @pl.when(depth_ref[0] < NSL - 1)
    def _():
        if not split:
            g_ref[...] = jnp.zeros_like(g_ref)
            return

        @pl.when(depth_ref[0] > 1)
        def _():
            both_ref[...] = kv_ref[...]

        @pl.when(depth_ref[0] <= 1)
        def _():
            both_ref[...] = other_ref[...]

        work(2 * size, (g_ref, next_ref), both_ref)


def piece(depth, rows_of, kv, other, dq, held, block, start, size):
    many, dh = rows_of[-1].shape
    split = block == 1
    args = (depth, *rows_of, kv) + (() if dq is None else (dq,)) + (() if held is None else (held,))
    if split and start == 0:
        args += (other,)
    gave = jax.ShapeDtypeStruct((size, 2 * dh), BF16)
    keys = 2 * size if split and start == 0 else size
    return pl.pallas_call(
        functools.partial(piece_kernel, many // kv.shape[0], dh**-0.5, block, start, dq is None),
        in_specs=[SMEM] + [VMEM] * (len(args) - 1),
        out_specs=[VMEM] * (3 if split and start == 0 else 2),
        out_shape=[jax.ShapeDtypeStruct((many, dh), F32), gave] + ([gave] if split and start == 0 else []),
        scratch_shapes=([pltpu.VMEM(kv.shape, BF16)] if split and start == 0 else [])
        + [pltpu.VMEM((dh, keys), F32), pltpu.VMEM((dh, keys), F32)],
        input_output_aliases=({} if dq is None else {8: 0}) | ({} if held is None else {9: 1}),
        compiler_params=params(24),
        cost_estimate=cost(many, size, 1, dh),
        name="piece",
    )(*args)


def place_kernel(rows, table_ref, depth_ref, *refs):
    ins, out_ref, sem = refs[: len(PIECES)], refs[-2], refs[-1]
    copies = []
    for i, (block, first, size) in enumerate(PIECES):
        slot = table_ref[block] if block > 1 else table_ref[jnp.where(depth_ref[0] > 1, block, 1 - block)]
        at = pl.multiple_of(slot * rows + first, 128)
        copies.append(pltpu.make_async_copy(ins[i], out_ref.at[pl.ds(at, size), :], sem.at[i]))
    for c in copies:
        c.start()
    for c in copies:
        c.wait()


def place(table, depth, parts, shape, rows):
    return pl.pallas_call(
        functools.partial(place_kernel, rows),
        in_specs=[SMEM, SMEM] + [VMEM] * len(parts),
        out_specs=HBM,
        out_shape=jax.ShapeDtypeStruct(shape, BF16),
        scratch_shapes=[pltpu.SemaphoreType.DMA((len(PIECES),))],
        compiler_params=params(4),
        name="place",
    )(table, depth, *parts)


def per_device(query, grad_output, log_total, offset, slice_keys, pool_keys, block_table):
    rows, _ = log_total.shape[1:]
    table = block_table[0]
    sections = lax.axis_size("section")
    half_axis = sections // 2
    group = sections // NSL
    depths = [NSL - 1 - layer // group % (NSL - 1) for layer in range(sections)]
    me = lax.axis_index("section")
    depth = (NSL - 1 - me // group % (NSL - 1)).astype(jnp.int32).reshape(1)
    partner = (me + half_axis) % sections
    partner_depth = (NSL - 1 - partner // group % (NSL - 1)).astype(jnp.int32).reshape(1)

    swap = [(layer, (layer + half_axis) % sections) for layer in range(sections)]
    home = [(layer, p) for layer, p in swap if depths[layer] == NSL - 1]
    deep = [(p, layer) for layer, p in swap if depths[layer] == NSL - 1]

    picked = pick(block_table, pool_keys[0], rows)
    arrived = {}
    for i, block in enumerate(BLOCKS):
        arrived[block] = lax.ppermute(picked[i], "section", deep if block == NSL - 2 else swap)
    rows_of = prep(query[0], grad_output[0], log_total[0].T, offset[0].T)
    dq = held = None
    parts = []
    for block, start, size in PIECES:
        dq, g, *rest = piece(depth, rows_of, arrived[block], arrived[0], dq, held, block, start, size)
        held = rest[0] if rest else None
        parts.append(lax.ppermute(g, "section", home if block == NSL - 2 else swap))
    query_grad, slice_grad = own(rows_of, slice_keys[0], dq)
    pool_grad = place(table, partner_depth, parts, pool_keys.shape[1:], rows)
    return (query_grad[None], slice_grad[None], pool_grad[None])


def solution(mesh):
    spec = P("section", None, "kv")
    return jax.shard_map(
        per_device,
        mesh=mesh,
        in_specs=(spec, spec, spec, spec, spec, spec, P("section", None)),
        out_specs=(spec, spec, spec),
        check_vma=False,
    )
```
